32 devices in a mesh: ctx: 8 (over z, y), ch: 4 (over x, core).
Axes of the slice: x: 2, y: 2, z: 4, core: 2. Of those that a mesh axis runs over, the one named last changes fastest.
Arguments:
- query_short: bfloat16 [2048, 8192], P('ctx', 'ch'), may hold values from -6 to 6
- key_short: bfloat16 [2048, 8192], P('ctx', 'ch'), may hold values from -6 to 6
- value_short: bfloat16 [2048, 8192], P('ctx', 'ch'), may hold values from -6 to 6
- grad_short: bfloat16 [2048, 8192], P('ctx', 'ch'), may hold values from -10 to 10
- query_medium: bfloat16 [2048, 8192], P('ctx', 'ch'), may hold values from -6 to 6
- key_medium: bfloat16 [2048, 8192], P('ctx', 'ch'), may hold values from -6 to 6
- value_medium: bfloat16 [2048, 8192], P('ctx', 'ch'), may hold values from -6 to 6
- grad_medium: bfloat16 [2048, 8192], P('ctx', 'ch'), may hold values from -10 to 10
- query_long: bfloat16 [2048, 8192], P('ctx', 'ch'), may hold values from -6 to 6
- key_long: bfloat16 [2048, 8192], P('ctx', 'ch'), may hold values from -8 to 8
- value_long: bfloat16 [2048, 8192], P('ctx', 'ch'), may hold values from -8 to 8
- grad_long: bfloat16 [2048, 8192], P('ctx', 'ch'), may hold values from -10 to 10
- taps_short: float32 [7, 8192], P(None, 'ch'), may hold values from -2 to 2
- taps_medium: float32 [128, 8192], P(None, 'ch'), may hold values from -0.5 to 0.5
- residues: float32 [16, 8192], P(None, 'ch'), may hold values from -1.5 to 1.5
- decay_rates: float32 [16, 8192], P(None, 'ch'), may hold values from 2.4414063e-05 to 0.07
Outputs:
- query_grad_short: bfloat16 [2048, 8192], P('ctx', 'ch')
- key_grad_short: bfloat16 [2048, 8192], P('ctx', 'ch')
- value_grad_short: bfloat16 [2048, 8192], P('ctx', 'ch')
- query_grad_medium: bfloat16 [2048, 8192], P('ctx', 'ch')
- key_grad_medium: bfloat16 [2048, 8192], P('ctx', 'ch')
- value_grad_medium: bfloat16 [2048, 8192], P('ctx', 'ch')
- query_grad_long: bfloat16 [2048, 8192], P('ctx', 'ch')
- key_grad_long: bfloat16 [2048, 8192], P('ctx', 'ch')
- value_grad_long: bfloat16 [2048, 8192], P('ctx', 'ch')
- taps_short_grad: float32 [7, 8192], P(None, 'ch')
- taps_medium_grad: float32 [128, 8192], P(None, 'ch')
- residue_grad: float32 [16, 8192], P(None, 'ch')
The draws below stay inside these ranges and needn't reach their ends.
All inputs are finite; a program needn't handle non-finite values.
Results may differ from the reference program's by a relative error of at most 0.008.
Values may be sent and summed in bfloat16 or wider, within the bound.
A program may use at most 128 MiB of HBM per device.

```python
import math
import jax
import jax.numpy as jnp
from jax import lax

C = 8192
TOK_DEV = 256
SE_LEN = 7
MR_LEN = 128
ORDER = 16
LENGTH = 2048


def base_noise(key, limit):
    return jnp.clip(jax.random.normal(key, (LENGTH, C), jnp.float32), -limit, limit)


def column_scales():
    columns = jnp.arange(C, dtype=jnp.float32) / (C - 1)
    return 0.1 * jnp.exp(math.log(10.0) * columns)


def block_envelope(late):
    places = (jnp.arange(LENGTH, dtype=jnp.int32) % TOK_DEV).astype(jnp.float32)
    if late:
        distance = (TOK_DEV - 1.0 - places) / TOK_DEV
    else:
        distance = places / TOK_DEV
    return (0.5 + 1.5 * jnp.exp(-5.0 * distance))[:, None]


def ramped_cotangent(key, salt):
    key = jax.random.fold_in(key, salt)
    first, second = jax.random.split(key)
    noise = base_noise(first, 6.0)
    offset = jax.random.uniform(second, (1, C), jnp.float32, 0.25, 0.5)
    ramp = (1.0 + 2.0 * jnp.arange(LENGTH, dtype=jnp.float32) / (LENGTH - 1))[:, None]
    values = (noise + offset * ramp) * column_scales()[None, :]
    return values.astype(jnp.bfloat16)


def offset_input(key, salt):
    key = jax.random.fold_in(key, salt)
    first, second = jax.random.split(key)
    noise = base_noise(first, 5.0)
    offset = jax.random.uniform(second, (1, C), jnp.float32, 0.25, 0.5)
    return (noise + offset).astype(jnp.bfloat16)


def shaped_input(key, salt):
    key = jax.random.fold_in(key, salt)
    noise = base_noise(key, 4.0)
    return (noise * block_envelope(False)).astype(jnp.bfloat16)


def draw_grad_short(key, part):
    return ramped_cotangent(key, 11)


def draw_grad_medium(key, part):
    return ramped_cotangent(key, 23)


def draw_grad_long(key, part):
    key = jax.random.fold_in(key, 37)
    noise = base_noise(key, 4.0)
    values = noise * block_envelope(True) * column_scales()[None, :]
    return values.astype(jnp.bfloat16)


def draw_query_short(key, part):
    return offset_input(key, 41)


def draw_key_short(key, part):
    return offset_input(key, 43)


def draw_value_short(key, part):
    return offset_input(key, 47)


def draw_query_medium(key, part):
    return offset_input(key, 53)


def draw_key_medium(key, part):
    return offset_input(key, 59)


def draw_value_medium(key, part):
    return offset_input(key, 61)


def draw_key_long(key, part):
    return shaped_input(key, 67)


def draw_value_long(key, part):
    return shaped_input(key, 71)


def draw_decay_rates(key, part):
    key = jax.random.fold_in(key, 79)
    keys = jax.random.split(key, 4)
    shape = (ORDER, C)
    pick = jax.random.uniform(keys[0], shape, jnp.float32)
    lowest = 0.05 / LENGTH
    slow_top = 2.0 / LENGTH
    band = jax.random.uniform(keys[2], shape, jnp.float32, 0.011, 0.0155)
    slow = jnp.exp(jax.random.uniform(keys[1], shape, jnp.float32, math.log(lowest), math.log(slow_top)))
    fast = jnp.exp(jax.random.uniform(keys[3], shape, jnp.float32, math.log(0.03), math.log(0.07)))
    cut_slow = 0.35
    cut_band = 0.68
    rates = jnp.where(pick < cut_slow, slow, jnp.where(pick < cut_band, band, fast))
    return jnp.clip(rates, lowest, 0.07)


def steps_of(rng, extent, cuts, smallest, largest):
    def one(position, shards_of):
        heights = jax.random.uniform(jax.random.fold_in(jax.random.fold_in(rng, 6), position), (shards_of,), jnp.float32, smallest / len(cuts), largest / len(cuts))
        return jnp.repeat(jnp.exp(heights), extent[position] // shards_of).reshape((-1,) + (1,) * (len(extent) - position - 1))

    level = one(*cuts[0])
    for cut in cuts[1:]:
        level = level * one(*cut)
    return level


def bell_draw(own_key, extent, scale, bound, cuts=(), kind=jnp.bfloat16):
    level = steps_of(own_key, extent, cuts, -0.22, 0.18) if cuts else 1.0
    values = jax.random.normal(own_key, extent, jnp.float32) * scale * level
    return jnp.minimum(jnp.maximum(values, -bound), bound).astype(kind)


def setup_inputs(seed: int = 0) -> dict:
    key_list = jax.random.split(jax.random.key(seed), 17)
    query_short = draw_query_short(jax.random.fold_in(key_list[16], 71), 0)
    key_short = draw_key_short(jax.random.fold_in(key_list[16], 71), 0)
    value_short = draw_value_short(jax.random.fold_in(key_list[16], 71), 0)
    grad_short = draw_grad_short(jax.random.fold_in(key_list[16], 71), 0)
    query_medium = draw_query_medium(jax.random.fold_in(key_list[16], 71), 0)
    key_medium = draw_key_medium(jax.random.fold_in(key_list[16], 71), 0)
    value_medium = draw_value_medium(jax.random.fold_in(key_list[16], 71), 0)
    grad_medium = draw_grad_medium(jax.random.fold_in(key_list[16], 71), 0)
    query_long = bell_draw(key_list[8], (LENGTH, C), 1.0, 6.0, ((0, 8), (1, 4)))
    key_long = draw_key_long(jax.random.fold_in(key_list[16], 71), 0)
    value_long = draw_value_long(jax.random.fold_in(key_list[16], 71), 0)
    grad_long = draw_grad_long(jax.random.fold_in(key_list[16], 71), 0)
    taps_short = bell_draw(key_list[12], (SE_LEN, C), SE_LEN ** -0.5, 2.0, ((1, 4),), jnp.float32)
    taps_medium = bell_draw(key_list[13], (MR_LEN, C), MR_LEN ** -0.5, 0.5, ((1, 4),), jnp.float32)
    residues = bell_draw(key_list[14], (ORDER, C), ORDER ** -0.5, 1.5, ((1, 4),), jnp.float32)
    decay_rates = draw_decay_rates(jax.random.fold_in(key_list[16], 71), 0)
    return dict(query_short=query_short, key_short=key_short, value_short=value_short, grad_short=grad_short, query_medium=query_medium, key_medium=key_medium, value_medium=value_medium, grad_medium=grad_medium, query_long=query_long, key_long=key_long, value_long=value_long, grad_long=grad_long, taps_short=taps_short, taps_medium=taps_medium, residues=residues, decay_rates=decay_rates)


def elementwise(first, second):
    return (first.astype(jnp.float32) * second.astype(jnp.float32)).astype(jnp.bfloat16)

def causal_pair(product, signal, taps):
    length = product.shape[0]
    size = 2 * length
    product_f = product.astype(jnp.float32)
    signal_f = signal.astype(jnp.float32)
    spec_taps = jnp.fft.rfft(taps, n=size, axis=0)
    spec_product = jnp.fft.rfft(product_f, n=size, axis=0)
    forward = jnp.fft.irfft(spec_product * spec_taps, n=size, axis=0)[:length]
    spec_reversed = jnp.fft.rfft(signal_f[::-1], n=size, axis=0)
    backward = jnp.fft.irfft(spec_reversed * spec_taps, n=size, axis=0)[:length][::-1]
    spec_signal = jnp.fft.rfft(signal_f, n=size, axis=0)
    lagged = jnp.fft.irfft(spec_signal * jnp.conj(spec_product), n=size, axis=0)
    return (forward, backward, lagged[:taps.shape[0]])

def explicit(product, signal, taps):
    length, width = product.shape
    groups = width // 128

    def split(array):
        return jnp.moveaxis(array.reshape(array.shape[0], groups, 128), 1, 0)

    def join(array):
        return jnp.moveaxis(array, 0, 1).reshape(array.shape[1], width)

    def one_group(pieces):
        return causal_pair(pieces[0], pieces[1], pieces[2])
    forward, backward, tap_sums = lax.map(one_group, (split(product), split(signal), split(taps)))
    return (join(forward), join(backward), join(tap_sums))

def long_modes(product, signal, residues, decay_rates):
    product_f = product.astype(jnp.float32)
    signal_f = signal.astype(jnp.float32)
    decay = jnp.exp(-decay_rates)
    amplitude = jnp.sqrt(-jnp.expm1(-2.0 * decay_rates))
    weight = amplitude * residues

    def forward_step(carry, row):
        state, accum = carry
        state = decay * state + row[0][None, :]
        accum = accum + row[1][None, :] * state
        return ((state, accum), lax.optimization_barrier(jnp.sum(weight * state, 0)))
    zeros = jnp.zeros(decay_rates.shape, jnp.float32)
    (last, accum), forward = lax.scan(forward_step, (zeros, zeros), (product_f, signal_f))

    def back_step(state, row):
        state = decay * state + row[None, :]
        return (state, lax.optimization_barrier(jnp.sum(weight * state, 0)))
    first, backward = lax.scan(back_step, zeros, signal_f, reverse=True)
    return (forward, backward, amplitude * accum)

def operator_grads(query, keys, values, grad, forward, backward):
    query_grad = (grad.astype(jnp.float32) * forward).astype(jnp.bfloat16)
    key_grad = (backward * values.astype(jnp.float32)).astype(jnp.bfloat16)
    value_grad = (backward * keys.astype(jnp.float32)).astype(jnp.bfloat16)
    return (query_grad, key_grad, value_grad)

def reference(query_short, key_short, value_short, grad_short, query_medium, key_medium, value_medium, grad_medium, query_long, key_long, value_long, grad_long, taps_short, taps_medium, residues, decay_rates):
    product_short = elementwise(key_short, value_short)
    product_medium = elementwise(key_medium, value_medium)
    product_long = elementwise(key_long, value_long)
    signal_short = elementwise(grad_short, query_short)
    signal_medium = elementwise(grad_medium, query_medium)
    signal_long = elementwise(grad_long, query_long)
    forward_short, backward_short, raw_short = explicit(product_short, signal_short, taps_short)
    forward_medium, backward_medium, raw_medium = explicit(product_medium, signal_medium, taps_medium)
    forward_long, backward_long, raw_residue = long_modes(product_long, signal_long, residues, decay_rates)
    grads_short = operator_grads(query_short, key_short, value_short, grad_short, forward_short, backward_short)
    grads_medium = operator_grads(query_medium, key_medium, value_medium, grad_medium, forward_medium, backward_medium)
    grads_long = operator_grads(query_long, key_long, value_long, grad_long, forward_long, backward_long)
    squares = jnp.sum(raw_short * raw_short) + jnp.sum(raw_medium * raw_medium) + jnp.sum(raw_residue * raw_residue)
    entries = (taps_short.shape[0] + taps_medium.shape[0] + residues.shape[0]) * residues.shape[1]
    factor = 1.0 / jnp.sqrt(squares / entries + 1e-06)
    return (grads_short[0], grads_short[1], grads_short[2], grads_medium[0], grads_medium[1], grads_medium[2], grads_long[0], grads_long[1], grads_long[2], factor * raw_short, factor * raw_medium, factor * raw_residue)
```

```python
import functools

import jax
import jax.numpy as jnp
import numpy as np
from jax import lax
from jax.experimental import pallas as pl
from jax.experimental.pallas import tpu as pltpu
from jax.sharding import PartitionSpec as P

F32 = jnp.float32
BF16 = jnp.bfloat16
HALO = 16
MESH = pl.DeviceIdType.MESH


def from_behind(value, axis, steps):
    count = lax.axis_size(axis)
    first, last = (max(0, -steps), min(count, count - steps))
    return lax.ppermute(value, axis, [(source, source + steps) for source in range(first, last)])


def elementwise(first, second):
    return (first.astype(F32) * second.astype(F32)).astype(BF16)


def hi_lo(array):
    high = array.astype(BF16)
    low = (array - high.astype(F32)).astype(BF16)
    return high, low


def transform(size, points):
    turns = np.outer(2 * np.arange(size // 2) + 1, np.arange(points)) % (2 * size)
    angle = np.pi * turns / size
    return np.concatenate([np.cos(angle), np.sin(angle)], 0)


def np_hi_lo(matrix):
    matrix = np.asarray(matrix, np.float32)
    high = matrix.astype(jnp.bfloat16)
    low = (matrix - high.astype(np.float32)).astype(jnp.bfloat16)
    return np.stack([high, low])


def mul(first, second):
    return jnp.dot(first, second, preferred_element_type=F32)


def spectrum(matrix, data):
    return mul(matrix[0], data) + mul(matrix[1], data)


def wide(matrix, data):
    high, low = hi_lo(data)
    return mul(matrix[0], high) + (mul(matrix[0], low) + mul(matrix[1], high))


def convolved(first, second):
    half = first.shape[0] // 2
    fr, fs, sr, ss = first[:half], first[half:], second[:half], second[half:]
    return jnp.concatenate([fr * sr - fs * ss, fr * ss + fs * sr], 0)


def correlated(first, second):
    half = first.shape[0] // 2
    fr, fs, sr, ss = first[:half], first[half:], second[:half], second[half:]
    return jnp.concatenate([fr * sr + fs * ss, fs * sr - fr * ss], 0)


def ladder(rates):
    steps = lax.broadcasted_iota(jnp.int32, (1, 8, 1), 1).astype(F32)
    return jnp.exp(-rates[:, None, :] * steps), jnp.exp(-8.0 * rates)


def long_local_kernel(
    q_ref, k_ref, v_ref, g_ref, w_ref, d_ref, f_ref, i_ref, fl_ref, bl_ref, st_ref, h_scr, p_scr, s_scr
):
    length, width = q_ref.shape
    modes = d_ref.shape[0]
    tiles = length // 8
    product = elementwise(k_ref[...], v_ref[...])
    signal = elementwise(g_ref[...], q_ref[...])
    p_scr[...] = product.astype(F32)
    s_scr[...] = signal.astype(F32)
    for lane in range(0, width, 128):
        cols = slice(lane, lane + 128)
        rates = d_ref[:, cols]
        powers, step = ladder(rates)
        step = jnp.broadcast_to(step[:, None, :], (modes, 8, 128))

        def filter_step(a, state):
            h_scr[pl.ds(pl.multiple_of(a * 8, 8), 8), cols] = jnp.sum(state, 0)
            return state * step

        lax.fori_loop(0, tiles, filter_step, powers * w_ref[:, cols][:, None, :], unroll=4)
    ps = spectrum(f_ref, product)
    ss = spectrum(f_ref, signal)
    hs = wide(f_ref, h_scr[...])
    fl_ref[...] = wide(i_ref, convolved(ps, hs))
    bl_ref[...] = wide(i_ref, correlated(ss, hs))
    h_scr[...] = wide(i_ref, correlated(ss, ps))
    for lane in range(0, width, 128):
        cols = slice(lane, lane + 128)
        rates = d_ref[:, cols]
        powers, step = ladder(rates)
        step = jnp.broadcast_to(step[:, None, :], (modes, 8, 128))
        steps = lax.broadcasted_iota(jnp.int32, (1, 8, 1), 1).astype(F32)
        falling = jnp.exp(-rates[:, None, :] * (7.0 - steps))
        zeros = jnp.zeros((modes, 8, 128), F32)

        def end_step(a, state):
            return state * step + p_scr[pl.ds(pl.multiple_of(a * 8, 8), 8), cols][None]

        def start_step(a, states):
            at = pl.ds(pl.multiple_of((tiles - 1 - a) * 8, 8), 8)
            return (states[0] * step + s_scr[at, cols][None], states[1] * step + h_scr[at, cols][None])

        ends = lax.fori_loop(0, tiles, end_step, zeros, unroll=4)
        st_ref[0:modes, cols] = jnp.sum(ends * falling, 1)
        starts, lags = lax.fori_loop(0, tiles, start_step, (zeros, zeros), unroll=4)
        st_ref[modes : 2 * modes, cols] = jnp.sum(starts * powers, 1)
        st_ref[2 * modes : 3 * modes, cols] = jnp.sum(lags * powers, 1)


def explicit_kernel(
    qs, ks, vs, gs, qm, km, vm, gm, before, after, ts, tm, f_ref, i_ref,
    qs_o, ks_o, vs_o, qm_o, km_o, vm_o, raw_ref,
):
    length = qs.shape[0]
    taps = ts.shape[0]
    lags = tm.shape[0]
    product = elementwise(ks[...], vs[...]).astype(F32)
    signal = elementwise(gs[...], qs[...]).astype(F32)
    padded = jnp.concatenate([before[0:HALO].astype(F32), product], 0)
    trailing = jnp.concatenate([signal, after[0:HALO].astype(F32)], 0)
    forward = ts[0:1] * product
    backward = ts[0:1] * signal
    raw_ref[0:8, :] = jnp.zeros((8, raw_ref.shape[1]), F32)
    raw_ref[0:1, :] = jnp.sum(signal * product, 0, keepdims=True)
    for j in range(1, taps):
        shifted = padded[HALO - j : HALO - j + length]
        forward = forward + ts[j : j + 1] * shifted
        raw_ref[j : j + 1, :] = jnp.sum(signal * shifted, 0, keepdims=True)
        backward = backward + ts[j : j + 1] * trailing[j : j + length]
    qs_o[...] = (gs[...].astype(F32) * forward).astype(BF16)
    ks_o[...] = (backward * vs[...].astype(F32)).astype(BF16)
    vs_o[...] = (backward * ks[...].astype(F32)).astype(BF16)

    product = elementwise(km[...], vm[...])
    signal = elementwise(gm[...], qm[...])
    near = f_ref[:, :, 0:length]
    far = f_ref[:, :, length : length + lags]
    own = spectrum(near, product)
    ps = own - spectrum(far, before[HALO : HALO + lags])
    ss = spectrum(near, signal) + spectrum(far, after[HALO : HALO + lags])
    hs = wide(f_ref[:, :, 0:lags], tm[...])
    forward = wide(i_ref, convolved(ps, hs))
    backward = wide(i_ref, correlated(ss, hs))
    raw_ref[8 : 8 + lags, :] = wide(i_ref[:, 0:lags], correlated(ss, own))
    qm_o[...] = (gm[...].astype(F32) * forward).astype(BF16)
    km_o[...] = (backward * vm[...].astype(F32)).astype(BF16)
    vm_o[...] = (backward * km[...].astype(F32)).astype(BF16)


def long_final_kernel(k_ref, v_ref, g_ref, fl_ref, bl_ref, w_ref, d_ref, c_ref, qo, ko, vo, f_scr, b_scr):
    length, width = k_ref.shape
    modes = d_ref.shape[0]
    tiles = length // 8
    for lane in range(0, width, 128):
        cols = slice(lane, lane + 128)
        rates = d_ref[:, cols]
        powers, step = ladder(rates)
        step = jnp.broadcast_to(step[:, None, :], (modes, 8, 128))
        steps = lax.broadcasted_iota(jnp.int32, (1, 8, 1), 1).astype(F32)
        falling = jnp.exp(-rates[:, None, :] * (7.0 - steps))
        scale = w_ref[:, cols] * jnp.exp(-rates)
        into = (scale * c_ref[0:modes, cols])[:, None, :] * powers
        back = (scale * c_ref[modes : 2 * modes, cols])[:, None, :] * falling

        def one(a, states):
            f_scr[pl.ds(pl.multiple_of(a * 8, 8), 8), cols] = jnp.sum(states[0], 0)
            b_scr[pl.ds(pl.multiple_of((tiles - 1 - a) * 8, 8), 8), cols] = jnp.sum(states[1], 0)
            return (states[0] * step, states[1] * step)

        lax.fori_loop(0, tiles, one, (into, back), unroll=4)
    backward = bl_ref[...] + b_scr[...]
    qo[...] = (g_ref[...].astype(F32) * (fl_ref[...] + f_scr[...])).astype(BF16)
    ko[...] = (backward * v_ref[...].astype(F32)).astype(BF16)
    vo[...] = (backward * k_ref[...].astype(F32)).astype(BF16)


def exchange_kernel(
    count, groups, owners, length, entries,
    st, raw, rates, amp,
    short_o, medium_o, residue_o, carry_o,
    in_st, in_raw, out_c, out_s, in_c, in_s, own_sq, in_sq,
    st_send, st_recv, raw_send, raw_recv, c_send, c_recv, s_send, s_recv, q_send, q_recv,
):
    me = lax.axis_index("ctx")
    group = lax.axis_index("ch")
    modes = rates.shape[0]
    lags = medium_o.shape[0]
    taps = short_o.shape[0]
    width = rates.shape[1] // owners

    def guarded(condition, action):
        if owners == count:
            action()
        else:
            pl.when(condition)(action)

    barrier = pltpu.get_barrier_semaphore()
    for k in range(1, count):
        pl.semaphore_signal(barrier, inc=1, device_id={"ctx": lax.rem(me + k, count)}, device_id_type=MESH)
    for k in range(1, groups):
        pl.semaphore_signal(barrier, inc=1, device_id={"ch": lax.rem(group + k, groups)}, device_id_type=MESH)
    pl.semaphore_wait(barrier, count + groups - 2)

    def send(source, target, k, send_sem, recv_sem):
        return pltpu.make_async_remote_copy(
            src_ref=source, dst_ref=target, send_sem=send_sem.at[k], recv_sem=recv_sem.at[k],
            device_id={"ctx": lax.rem(me + k, count)}, device_id_type=MESH,
        )

    def chunk(owner):
        return pl.ds(pl.multiple_of(owner * width, 128), width)

    def gathered(k, slot):
        to = lax.rem(me + k, count)
        return (
            send(st.at[:, chunk(to)], in_st.at[slot], k, st_send, st_recv),
            send(raw.at[:, chunk(to)], in_raw.at[slot], k, raw_send, raw_recv),
        )

    def returned(k, slot, sums):
        to = lax.rem(me + k, count)
        if sums:
            return send(out_s, in_s.at[slot], k, s_send, s_recv)
        return send(out_c.at[to], in_c.at[slot], k, c_send, c_recv)

    for k in range(1, count):
        def start_one(k=k):
            for copy in gathered(k, me):
                copy.start()
        guarded(lax.rem(me + k, count) < owners, start_one)

    def own():
        in_st[me] = st[:, chunk(me)]
        in_raw[me] = raw[:, chunk(me)]
        for k in range(1, count):
            for copy in gathered(k, lax.rem(me + count - k, count)):
                copy.wait_recv()
        rate = rates[:, chunk(me)]
        fade = jnp.exp(-rate)
        over = jnp.exp(-float(length) * rate)
        carry = jnp.zeros(rate.shape, F32)
        residue = jnp.zeros(rate.shape, F32)
        for i in range(count):
            out_c[i, 0:modes] = carry
            starts = in_st[i, modes : 2 * modes]
            residue = residue + in_st[i, 2 * modes : 3 * modes] + carry * fade * starts
            carry = carry * over + in_st[i, 0:modes]
        carry = jnp.zeros(rate.shape, F32)
        for i in reversed(range(count)):
            out_c[i, modes : 2 * modes] = carry
            carry = carry * over + in_st[i, modes : 2 * modes]
        sums = in_raw[0]
        for i in range(1, count):
            sums = sums + in_raw[i]
        residue = residue * amp[:, chunk(me)]
        square = jnp.sum(jnp.sum(sums * sums, 0, keepdims=True), 1, keepdims=True) + jnp.sum(
            jnp.sum(residue * residue, 0, keepdims=True), 1, keepdims=True
        )
        square = jnp.broadcast_to(square, (8, width))
        for i in range(count):
            out_c[i, 2 * modes : 2 * modes + 8] = square
        out_s[...] = jnp.concatenate([sums, residue, jnp.zeros((8, width), F32)], 0).astype(BF16)
        for k in range(1, count):
            returned(k, me, False).start()
        for k in range(1, count):
            returned(k, me, True).start()
        in_c[me] = out_c[me]
        in_s[me] = out_s[...]

    guarded(me < owners, own)

    for k in range(1, count):
        source = lax.rem(me + count - k, count)
        def wait_carry(k=k, source=source):
            returned(k, source, False).wait_recv()
        guarded(source < owners, wait_carry)
    total = in_c[0, 2 * modes : 2 * modes + 8]
    for i in range(1, owners):
        total = total + in_c[i, 2 * modes : 2 * modes + 8]
    own_sq[...] = total
    in_sq[group] = total

    def shared(k, slot):
        return pltpu.make_async_remote_copy(
            src_ref=own_sq, dst_ref=in_sq.at[slot], send_sem=q_send.at[k], recv_sem=q_recv.at[k],
            device_id={"ch": lax.rem(group + k, groups)}, device_id_type=MESH,
        )

    for k in range(1, groups):
        shared(k, group).start()
    for i in range(owners):
        carry_o[:, i * width : (i + 1) * width] = in_c[i, 0 : 2 * modes]
    for k in range(1, count):
        source = lax.rem(me + count - k, count)
        def wait_sums(k=k, source=source):
            returned(k, source, True).wait_recv()
        guarded(source < owners, wait_sums)
    for k in range(1, groups):
        shared(k, lax.rem(group + groups - k, groups)).wait_recv()
    total = in_sq[0]
    for i in range(1, groups):
        total = total + in_sq[i]
    factor = (1.0 / jnp.sqrt(total / entries + 1e-06))[0:1]
    for i in range(owners):
        cols = slice(i * width, (i + 1) * width)
        block = in_s[i].astype(F32) * factor
        short_o[:, cols] = block[0:taps]
        medium_o[:, cols] = block[8 : 8 + lags]
        residue_o[:, cols] = block[8 + lags : 8 + lags + modes]
    for k in range(1, count):
        def wait_gather(k=k):
            for copy in gathered(k, me):
                copy.wait_send()
        guarded(lax.rem(me + k, count) < owners, wait_gather)
        def wait_return(k=k):
            returned(k, me, False).wait_send()
            returned(k, me, True).wait_send()
        guarded(me < owners, wait_return)
    for k in range(1, groups):
        shared(k, group).wait_send()


def exchange(st, raw, rates, amp, taps, lags, length):
    count, groups = lax.axis_size("ctx"), lax.axis_size("ch")
    modes, wide_c = rates.shape
    owners = min(count, wide_c // 128)
    width = wide_c // owners
    rows = raw.shape[0]
    entries = float((taps + lags + modes) * wide_c * groups)
    dma = pltpu.SemaphoreType.DMA
    vmem = pl.BlockSpec(memory_space=pltpu.VMEM)
    return pl.pallas_call(
        functools.partial(exchange_kernel, count, groups, owners, length, entries),
        out_shape=[
            jax.ShapeDtypeStruct((taps, wide_c), F32),
            jax.ShapeDtypeStruct((lags, wide_c), F32),
            jax.ShapeDtypeStruct((modes, wide_c), F32),
            jax.ShapeDtypeStruct((2 * modes, wide_c), F32),
        ],
        in_specs=[vmem] * 4,
        out_specs=[vmem] * 4,
        scratch_shapes=[
            pltpu.VMEM((count, 3 * modes, width), F32),
            pltpu.VMEM((count, rows, width), F32),
            pltpu.VMEM((count, 2 * modes + 8, width), F32),
            pltpu.VMEM((rows + modes + 8, width), BF16),
            pltpu.VMEM((owners, 2 * modes + 8, width), F32),
            pltpu.VMEM((owners, rows + modes + 8, width), BF16),
            pltpu.VMEM((8, width), F32),
            pltpu.VMEM((groups, 8, width), F32),
        ]
        + [dma((count,))] * 8
        + [dma((groups,))] * 2,
        compiler_params=pltpu.CompilerParams(
            collective_id=0, has_side_effects=True, vmem_limit_bytes=48 << 20
        ),
    )(st, raw, rates, amp)


def body(
    query_short, key_short, value_short, grad_short,
    query_medium, key_medium, value_medium, grad_medium,
    query_long, key_long, value_long, grad_long,
    taps_short, taps_medium, residues, decay_rates,
):
    length, channels = query_short.shape
    taps, lags, modes = taps_short.shape[0], taps_medium.shape[0], residues.shape[0]
    block = 256
    grid = (channels // block,)
    tails = jnp.concatenate(
        [
            elementwise(key_short[length - HALO :], value_short[length - HALO :]),
            elementwise(key_medium[length - lags :], value_medium[length - lags :]),
        ],
        0,
    )
    heads = jnp.concatenate(
        [
            elementwise(grad_short[:HALO], query_short[:HALO]),
            elementwise(grad_medium[:lags], query_medium[:lags]),
        ],
        0,
    )
    before = from_behind(tails, "ctx", 1)
    after = from_behind(heads, "ctx", -1)
    amplitudes = jnp.sqrt(-jnp.expm1(-2.0 * decay_rates))
    weights = amplitudes * residues

    def cols(rows):
        return pl.BlockSpec((rows, block), lambda i: (0, i))

    def const(shape):
        return pl.BlockSpec(shape, lambda i: (0,) * len(shape))

    def shape(rows, dtype):
        return jax.ShapeDtypeStruct((rows, channels), dtype)

    params = pltpu.CompilerParams(dimension_semantics=("arbitrary",), vmem_limit_bytes=48 << 20)
    full = 2 * length
    long_f = np_hi_lo(transform(full, length))
    long_i = np_hi_lo(transform(full, length).T * (2.0 / full))
    fl, bl, st = pl.pallas_call(
        long_local_kernel,
        grid=grid,
        in_specs=[cols(length)] * 4 + [cols(modes)] * 2 + [const(long_f.shape), const(long_i.shape)],
        out_specs=[cols(length), cols(length), cols(3 * modes)],
        out_shape=[shape(length, F32), shape(length, F32), shape(3 * modes, F32)],
        scratch_shapes=[pltpu.VMEM((length, block), F32)] * 3,
        compiler_params=params,
        cost_estimate=pl.CostEstimate(flops=20_000_000_000, bytes_accessed=8_000_000, transcendentals=0),
    )(query_long, key_long, value_long, grad_long, weights, decay_rates, jnp.asarray(long_f), jnp.asarray(long_i))

    part = length + lags
    part_f = np_hi_lo(transform(part, part))
    part_i = np_hi_lo(transform(part, length).T * (2.0 / part))
    outs = pl.pallas_call(
        explicit_kernel,
        grid=grid,
        in_specs=[cols(length)] * 8
        + [cols(HALO + lags)] * 2
        + [cols(taps), cols(lags), const(part_f.shape), const(part_i.shape)],
        out_specs=[cols(length)] * 6 + [cols(8 + lags)],
        out_shape=[shape(length, BF16)] * 6 + [shape(8 + lags, F32)],
        compiler_params=params,
        cost_estimate=pl.CostEstimate(flops=20_000_000_000, bytes_accessed=16_000_000, transcendentals=0),
    )(
        query_short, key_short, value_short, grad_short,
        query_medium, key_medium, value_medium, grad_medium,
        before, after, taps_short, taps_medium, jnp.asarray(part_f), jnp.asarray(part_i),
    )
    short_g, medium_g, residue_g, carries = exchange(
        st, outs[6], decay_rates, amplitudes, taps, lags, length
    )
    long_outs = pl.pallas_call(
        long_final_kernel,
        grid=grid,
        in_specs=[cols(length)] * 5 + [cols(modes)] * 2 + [cols(2 * modes)],
        out_specs=[cols(length)] * 3,
        out_shape=[shape(length, BF16)] * 3,
        scratch_shapes=[pltpu.VMEM((length, block), F32)] * 2,
        compiler_params=params,
        cost_estimate=pl.CostEstimate(flops=1_000_000_000, bytes_accessed=10_000_000, transcendentals=0),
    )(key_long, value_long, grad_long, fl, bl, weights, decay_rates, carries)
    return (*outs[:6], *long_outs, short_g, medium_g, residue_g)


def solution(mesh):
    tokens, filters = P("ctx", "ch"), P(None, "ch")
    return jax.shard_map(
        body,
        mesh=mesh,
        in_specs=(tokens,) * 12 + (filters,) * 4,
        out_specs=(tokens,) * 9 + (filters,) * 3,
        check_vma=False,
    )
```

```python
import functools

import jax
import jax.numpy as jnp
import numpy as np
from jax import lax
from jax.experimental import pallas as pl
from jax.experimental.pallas import tpu as pltpu
from jax.sharding import PartitionSpec as P

F32 = jnp.float32
BF16 = jnp.bfloat16
HALO = 16
MESH = pl.DeviceIdType.MESH


def from_behind(value, axis, steps):
    count = lax.axis_size(axis)
    first, last = (max(0, -steps), min(count, count - steps))
    return lax.ppermute(value, axis, [(source, source + steps) for source in range(first, last)])


def elementwise(first, second):
    return (first.astype(F32) * second.astype(F32)).astype(BF16)


def hi_lo(array):
    high = array.astype(BF16)
    low = (array - high.astype(F32)).astype(BF16)
    return high, low


def transform(size, points):
    turns = np.outer(2 * np.arange(size // 2) + 1, np.arange(points)) % (2 * size)
    angle = np.pi * turns / size
    return np.concatenate([np.cos(angle), np.sin(angle)], 0)


def np_hi_lo(matrix):
    matrix = np.asarray(matrix, np.float32)
    high = matrix.astype(jnp.bfloat16)
    low = (matrix - high.astype(np.float32)).astype(jnp.bfloat16)
    return np.stack([high, low])


def mul(first, second):
    return jnp.dot(first, second, preferred_element_type=F32)


def spectrum(matrix, data):
    return mul(matrix[0], data) + mul(matrix[1], data)


def wide(matrix, data):
    high, low = hi_lo(data)
    return mul(matrix[0], high) + (mul(matrix[0], low) + mul(matrix[1], high))


def inverse(matrix, data):
    high, low = hi_lo(data)
    return mul(matrix, high) + mul(matrix, low)


def convolved(first, second):
    half = first.shape[0] // 2
    fr, fs, sr, ss = first[:half], first[half:], second[:half], second[half:]
    return jnp.concatenate([fr * sr - fs * ss, fr * ss + fs * sr], 0)


def correlated(first, second):
    half = first.shape[0] // 2
    fr, fs, sr, ss = first[:half], first[half:], second[:half], second[half:]
    return jnp.concatenate([fr * sr + fs * ss, fs * sr - fr * ss], 0)


def ladder(rates):
    steps = lax.broadcasted_iota(jnp.int32, (1, 8, 1), 1).astype(F32)
    return jnp.exp(-rates[:, None, :] * steps), jnp.exp(-8.0 * rates)


def long_local_kernel(
    q_ref, k_ref, v_ref, g_ref, w_ref, d_ref, f_ref, i_ref, fl_ref, bl_ref, st_ref, h_scr, p_scr, s_scr
):
    length, width = q_ref.shape
    modes = d_ref.shape[0]
    tiles = length // 8
    product = elementwise(k_ref[...], v_ref[...])
    signal = elementwise(g_ref[...], q_ref[...])
    p_scr[...] = product.astype(F32)
    s_scr[...] = signal.astype(F32)
    for lane in range(0, width, 128):
        cols = slice(lane, lane + 128)
        rates = d_ref[:, cols]
        powers, step = ladder(rates)
        step = jnp.broadcast_to(step[:, None, :], (modes, 8, 128))

        def filter_step(a, state):
            h_scr[pl.ds(pl.multiple_of(a * 8, 8), 8), cols] = jnp.sum(state, 0)
            return state * step

        lax.fori_loop(0, tiles, filter_step, powers * w_ref[:, cols][:, None, :], unroll=4)
    ps = spectrum(f_ref, product)
    ss = spectrum(f_ref, signal)
    hs = wide(f_ref, h_scr[...])
    fl_ref[...] = inverse(i_ref[...], convolved(ps, hs))
    bl_ref[...] = inverse(i_ref[...], correlated(ss, hs))
    h_scr[...] = inverse(i_ref[...], correlated(ss, ps))
    for lane in range(0, width, 128):
        cols = slice(lane, lane + 128)
        rates = d_ref[:, cols]
        powers, step = ladder(rates)
        step = jnp.broadcast_to(step[:, None, :], (modes, 8, 128))
        steps = lax.broadcasted_iota(jnp.int32, (1, 8, 1), 1).astype(F32)
        falling = jnp.exp(-rates[:, None, :] * (7.0 - steps))
        zeros = jnp.zeros((modes, 8, 128), F32)

        def end_step(a, state):
            return state * step + p_scr[pl.ds(pl.multiple_of(a * 8, 8), 8), cols][None]

        def start_step(a, states):
            at = pl.ds(pl.multiple_of((tiles - 1 - a) * 8, 8), 8)
            return (states[0] * step + s_scr[at, cols][None], states[1] * step + h_scr[at, cols][None])

        ends = lax.fori_loop(0, tiles, end_step, zeros, unroll=4)
        st_ref[0:modes, cols] = jnp.sum(ends * falling, 1)
        starts, lags = lax.fori_loop(0, tiles, start_step, (zeros, zeros), unroll=4)
        st_ref[modes : 2 * modes, cols] = jnp.sum(starts * powers, 1)
        st_ref[2 * modes : 3 * modes, cols] = jnp.sum(lags * powers, 1)


def explicit_kernel(
    qs, ks, vs, gs, qm, km, vm, gm, before, after, ts, tm, f_ref, i_ref,
    qs_o, ks_o, vs_o, qm_o, km_o, vm_o, raw_ref,
):
    length = qs.shape[0]
    taps = ts.shape[0]
    lags = tm.shape[0]
    product = elementwise(ks[...], vs[...]).astype(F32)
    signal = elementwise(gs[...], qs[...]).astype(F32)
    padded = jnp.concatenate([before[0:HALO].astype(F32), product], 0)
    trailing = jnp.concatenate([signal, after[0:HALO].astype(F32)], 0)
    forward = ts[0:1] * product
    backward = ts[0:1] * signal
    sums = [jnp.sum(signal * product, 0, keepdims=True)]
    for j in range(1, taps):
        shifted = padded[HALO - j : HALO - j + length]
        forward = forward + ts[j : j + 1] * shifted
        sums.append(jnp.sum(signal * shifted, 0, keepdims=True))
        backward = backward + ts[j : j + 1] * trailing[j : j + length]
    sums.append(jnp.zeros((HALO - taps, sums[0].shape[1]), F32))
    raw_ref[0:HALO, :] = jnp.concatenate(sums, 0).astype(BF16)
    qs_o[...] = (gs[...].astype(F32) * forward).astype(BF16)
    ks_o[...] = (backward * vs[...].astype(F32)).astype(BF16)
    vs_o[...] = (backward * ks[...].astype(F32)).astype(BF16)

    product = elementwise(km[...], vm[...])
    signal = elementwise(gm[...], qm[...])
    near = f_ref[:, :, 0:length]
    far = f_ref[:, :, length : length + lags]
    own = spectrum(near, product)
    ps = own - spectrum(far, before[HALO : HALO + lags])
    ss = spectrum(near, signal) + spectrum(far, after[HALO : HALO + lags])
    hs = wide(f_ref[:, :, 0:lags], tm[...])
    forward = inverse(i_ref[...], convolved(ps, hs))
    backward = inverse(i_ref[...], correlated(ss, hs))
    raw_ref[HALO : HALO + lags, :] = inverse(i_ref[0:lags], correlated(ss, own)).astype(BF16)
    qm_o[...] = (gm[...].astype(F32) * forward).astype(BF16)
    km_o[...] = (backward * vm[...].astype(F32)).astype(BF16)
    vm_o[...] = (backward * km[...].astype(F32)).astype(BF16)


def long_final_kernel(
    early, k_ref, v_ref, g_ref, fl_a, fl_b, bl_a, bl_b, w_ref, d_ref, c_ref, qo, ko, vo, f_scr, b_scr
):
    length, width = k_ref.shape
    modes = d_ref.shape[0]
    tiles = length // 8
    for lane in range(0, width, 128):
        cols = slice(lane, lane + 128)
        rates = d_ref[:, cols]
        powers, step = ladder(rates)
        step = jnp.broadcast_to(step[:, None, :], (modes, 8, 128))
        steps = lax.broadcasted_iota(jnp.int32, (1, 8, 1), 1).astype(F32)
        falling = jnp.exp(-rates[:, None, :] * (7.0 - steps))
        scale = w_ref[:, cols] * jnp.exp(-rates)
        into = (scale * c_ref[0:modes, cols])[:, None, :] * powers
        back = (scale * c_ref[modes : 2 * modes, cols])[:, None, :] * falling

        def one(a, states):
            f_scr[pl.ds(pl.multiple_of(a * 8, 8), 8), cols] = jnp.sum(states[0], 0)
            b_scr[pl.ds(pl.multiple_of((tiles - 1 - a) * 8, 8), 8), cols] = jnp.sum(states[1], 0)
            return (states[0] * step, states[1] * step)

        lax.fori_loop(0, tiles, one, (into, back), unroll=4)

    def finish(fl_ref, bl_ref):
        backward = bl_ref[...] + b_scr[...]
        qo[...] = (g_ref[...].astype(F32) * (fl_ref[...] + f_scr[...])).astype(BF16)
        ko[...] = (backward * v_ref[...].astype(F32)).astype(BF16)
        vo[...] = (backward * k_ref[...].astype(F32)).astype(BF16)

    first = pl.program_id(0) < early
    pl.when(first)(lambda: finish(fl_a, bl_a))
    pl.when(jnp.logical_not(first))(lambda: finish(fl_b, bl_b))


def guarded(always, condition, action):
    if always:
        action()
    else:
        pl.when(condition)(action)


def chunk(owner, width):
    return pl.ds(pl.multiple_of(owner * width, 128), width)


def peer_copy(source, target, k, send_sem, recv_sem, count, me):
    return pltpu.make_async_remote_copy(
        src_ref=source, dst_ref=target, send_sem=send_sem.at[k], recv_sem=recv_sem.at[k],
        device_id={"ctx": lax.rem(me + k, count)}, device_id_type=MESH,
    )


def long_sums_kernel(
    count, owners,
    q_ref, k_ref, v_ref, g_ref, w_ref, d_ref, f_ref, i_ref, raw,
    fl_ref, bl_ref, st_ref, sums_o, square_o,
    h_scr, p_scr, s_scr, in_raw, total_s, in_s,
    own_sem, raw_send, raw_recv, s_send, s_recv,
):
    me = lax.axis_index("ctx")
    step, steps = pl.program_id(0), pl.num_programs(0)
    width = in_raw.shape[2]
    every = owners == count

    def gathered(k, slot):
        source = raw.at[:, chunk(lax.rem(me + k, count), width)]
        return peer_copy(source, in_raw.at[slot], k, raw_send, raw_recv, count, me)

    def returned(k, slot):
        return peer_copy(total_s, in_s.at[slot], k, s_send, s_recv, count, me)

    def kept():
        return pltpu.make_async_copy(raw.at[:, chunk(me, width)], in_raw.at[me], own_sem)

    @pl.when(step == 0)
    def _():
        barrier = pltpu.get_barrier_semaphore()
        for k in range(1, count):
            pl.semaphore_signal(barrier, inc=1, device_id={"ctx": lax.rem(me + k, count)}, device_id_type=MESH)
        pl.semaphore_wait(barrier, count - 1)
        for k in range(1, count):
            guarded(every, lax.rem(me + k, count) < owners, lambda k=k: gathered(k, me).start())
        guarded(every, me < owners, lambda: kept().start())

    @pl.when(step == steps // 2)
    def _():
        def own():
            kept().wait()
            for k in range(1, count):
                gathered(k, lax.rem(me + count - k, count)).wait_recv()
            sums = in_raw[0].astype(F32)
            for i in range(1, count):
                sums = sums + in_raw[i].astype(F32)
            square = jnp.sum(jnp.sum(sums * sums, 0, keepdims=True), 1, keepdims=True)
            square_o[...] = jnp.broadcast_to(square, square_o.shape)
            total_s[...] = sums.astype(BF16)
            for k in range(1, count):
                returned(k, me).start()
            in_s[me] = total_s[...]

        if not every:
            square_o[...] = jnp.zeros(square_o.shape, F32)
        guarded(every, me < owners, own)

    long_local_kernel(
        q_ref, k_ref, v_ref, g_ref, w_ref, d_ref, f_ref, i_ref, fl_ref, bl_ref, st_ref, h_scr, p_scr, s_scr
    )

    @pl.when(step == steps - 1)
    def _():
        for k in range(1, count):
            source = lax.rem(me + count - k, count)
            guarded(every, source < owners, lambda k=k, source=source: returned(k, source).wait_recv())
        sums_o[...] = in_s[...]
        for k in range(1, count):
            guarded(every, lax.rem(me + k, count) < owners, lambda k=k: gathered(k, me).wait_send())
            guarded(every, me < owners, lambda k=k: returned(k, me).wait_send())


def exchange_kernel(
    count, groups, owners, length, entries,
    st, sums, square, rates, amp,
    short_o, medium_o, residue_o, carry_o,
    in_st, out_c, in_c, own_sq, in_sq,
    st_send, st_recv, c_send, c_recv, q_send, q_recv,
):
    me = lax.axis_index("ctx")
    group = lax.axis_index("ch")
    modes = rates.shape[0]
    lags = medium_o.shape[0]
    taps = short_o.shape[0]
    width = in_st.shape[2]
    every = owners == count

    barrier = pltpu.get_barrier_semaphore()
    for k in range(1, count):
        pl.semaphore_signal(barrier, inc=1, device_id={"ctx": lax.rem(me + k, count)}, device_id_type=MESH)
    for k in range(1, groups):
        pl.semaphore_signal(barrier, inc=1, device_id={"ch": lax.rem(group + k, groups)}, device_id_type=MESH)
    pl.semaphore_wait(barrier, count + groups - 2)

    def gathered(k, slot):
        source = st.at[:, chunk(lax.rem(me + k, count), width)]
        return peer_copy(source, in_st.at[slot], k, st_send, st_recv, count, me)

    def returned(k, slot):
        return peer_copy(out_c.at[lax.rem(me + k, count)], in_c.at[slot], k, c_send, c_recv, count, me)

    for k in range(1, count):
        guarded(every, lax.rem(me + k, count) < owners, lambda k=k: gathered(k, me).start())

    def own():
        in_st[me] = st[:, chunk(me, width)]
        rate = rates[:, chunk(me, width)]
        fade = jnp.exp(-rate)
        over = jnp.exp(-float(length) * rate)
        for k in range(1, count):
            gathered(k, lax.rem(me + count - k, count)).wait_recv()
        carry = jnp.zeros(rate.shape, F32)
        residue = jnp.zeros(rate.shape, F32)
        for i in range(count):
            out_c[i, 0:modes] = carry
            starts = in_st[i, modes : 2 * modes]
            residue = residue + in_st[i, 2 * modes : 3 * modes] + carry * fade * starts
            carry = carry * over + in_st[i, 0:modes]
        carry = jnp.zeros(rate.shape, F32)
        for i in reversed(range(count)):
            out_c[i, modes : 2 * modes] = carry
            carry = carry * over + in_st[i, modes : 2 * modes]
        residue = residue * amp[:, chunk(me, width)]
        total = jnp.sum(jnp.sum(residue * residue, 0, keepdims=True), 1, keepdims=True)
        total = jnp.broadcast_to(total, (8, width)) + square[...]
        for i in range(count):
            out_c[i, 2 * modes : 3 * modes] = residue
            out_c[i, 3 * modes : 3 * modes + 8] = total
        for k in range(1, count):
            returned(k, me).start()
        in_c[me] = out_c[me]

    guarded(every, me < owners, own)

    for k in range(1, count):
        source = lax.rem(me + count - k, count)
        guarded(every, source < owners, lambda k=k, source=source: returned(k, source).wait_recv())
    total = in_c[0, 3 * modes : 3 * modes + 8]
    for i in range(1, owners):
        total = total + in_c[i, 3 * modes : 3 * modes + 8]
    own_sq[...] = total
    in_sq[group] = total

    def shared(k, slot):
        return pltpu.make_async_remote_copy(
            src_ref=own_sq, dst_ref=in_sq.at[slot], send_sem=q_send.at[k], recv_sem=q_recv.at[k],
            device_id={"ch": lax.rem(group + k, groups)}, device_id_type=MESH,
        )

    for k in range(1, groups):
        shared(k, group).start()
    for i in range(owners):
        carry_o[:, i * width : (i + 1) * width] = in_c[i, 0 : 2 * modes]
    for k in range(1, groups):
        shared(k, lax.rem(group + groups - k, groups)).wait_recv()
    total = in_sq[0]
    for i in range(1, groups):
        total = total + in_sq[i]
    factor = (1.0 / jnp.sqrt(total / entries + 1e-06))[0:1]
    for i in range(owners):
        cols = slice(i * width, (i + 1) * width)
        block = sums[i].astype(F32) * factor
        short_o[:, cols] = block[0:taps]
        medium_o[:, cols] = block[HALO : HALO + lags]
        residue_o[:, cols] = in_c[i, 2 * modes : 3 * modes] * factor
    for k in range(1, count):
        guarded(every, lax.rem(me + k, count) < owners, lambda k=k: gathered(k, me).wait_send())
        guarded(every, me < owners, lambda k=k: returned(k, me).wait_send())
    for k in range(1, groups):
        shared(k, group).wait_send()


def exchange(st, sums, square, rates, amp, taps, lags, length):
    count, groups = lax.axis_size("ctx"), lax.axis_size("ch")
    modes, wide_c = rates.shape
    owners, _, width = sums.shape
    entries = float((taps + lags + modes) * wide_c * groups)
    dma = pltpu.SemaphoreType.DMA
    vmem = pl.BlockSpec(memory_space=pltpu.VMEM)
    return pl.pallas_call(
        functools.partial(exchange_kernel, count, groups, owners, length, entries),
        out_shape=[
            jax.ShapeDtypeStruct((taps, wide_c), F32),
            jax.ShapeDtypeStruct((lags, wide_c), F32),
            jax.ShapeDtypeStruct((modes, wide_c), F32),
            jax.ShapeDtypeStruct((2 * modes, wide_c), F32),
        ],
        in_specs=[vmem] * 5,
        out_specs=[vmem] * 4,
        scratch_shapes=[
            pltpu.VMEM((count, 3 * modes, width), F32),
            pltpu.VMEM((count, 3 * modes + 8, width), F32),
            pltpu.VMEM((owners, 3 * modes + 8, width), F32),
            pltpu.VMEM((8, width), F32),
            pltpu.VMEM((groups, 8, width), F32),
        ]
        + [dma((count,))] * 4
        + [dma((groups,))] * 2,
        compiler_params=pltpu.CompilerParams(
            collective_id=0, has_side_effects=True, vmem_limit_bytes=48 << 20
        ),
    )(st, sums, square, rates, amp)


def body(
    query_short, key_short, value_short, grad_short,
    query_medium, key_medium, value_medium, grad_medium,
    query_long, key_long, value_long, grad_long,
    taps_short, taps_medium, residues, decay_rates,
):
    length, channels = query_short.shape
    taps, lags, modes = taps_short.shape[0], taps_medium.shape[0], residues.shape[0]
    block = 256
    grid = (channels // block,)
    tails = jnp.concatenate(
        [
            elementwise(key_short[length - HALO :], value_short[length - HALO :]),
            elementwise(key_medium[length - lags :], value_medium[length - lags :]),
        ],
        0,
    )
    heads = jnp.concatenate(
        [
            elementwise(grad_short[:HALO], query_short[:HALO]),
            elementwise(grad_medium[:lags], query_medium[:lags]),
        ],
        0,
    )
    before = from_behind(tails, "ctx", 1)
    after = from_behind(heads, "ctx", -1)
    amplitudes = jnp.sqrt(-jnp.expm1(-2.0 * decay_rates))
    weights = amplitudes * residues

    def cols(rows):
        return pl.BlockSpec((rows, block), lambda i: (0, i))

    def const(shape):
        return pl.BlockSpec(shape, lambda i: (0,) * len(shape))

    def shape(rows, dtype):
        return jax.ShapeDtypeStruct((rows, channels), dtype)

    params = pltpu.CompilerParams(dimension_semantics=("arbitrary",), vmem_limit_bytes=48 << 20)
    full = 2 * length
    long_f = np_hi_lo(transform(full, length))
    long_i = np.asarray(transform(full, length).T * (2.0 / full), np.float32).astype(BF16)
    long_in = (
        query_long, key_long, value_long, grad_long, weights, decay_rates, jnp.asarray(long_f), jnp.asarray(long_i)
    )
    steps = channels // block
    early = steps * 3 // 8
    late = steps - early

    def part_cols(rows, first):
        return pl.BlockSpec((rows, block), lambda i: (0, i + first))

    def long_specs(first):
        return (
            [part_cols(length, first)] * 4
            + [part_cols(modes, first)] * 2
            + [const(long_f.shape), const(long_i.shape)]
        )

    def long_shapes(number):
        return [
            jax.ShapeDtypeStruct((rows, number * block), F32) for rows in (length, length, 3 * modes)
        ]

    long_scratch = [pltpu.VMEM((length, block), F32)] * 3
    fl_a, bl_a, st_a = pl.pallas_call(
        long_local_kernel,
        grid=(early,),
        in_specs=long_specs(0),
        out_specs=[cols(length), cols(length), cols(3 * modes)],
        out_shape=long_shapes(early),
        scratch_shapes=long_scratch,
        compiler_params=params,
        cost_estimate=pl.CostEstimate(flops=10_000_000_000, bytes_accessed=4_000_000, transcendentals=0),
    )(*long_in)

    part = length + lags
    part_f = np_hi_lo(transform(part, part))
    part_i = np.asarray(transform(part, length).T * (2.0 / part), np.float32).astype(BF16)
    outs = pl.pallas_call(
        explicit_kernel,
        grid=grid,
        in_specs=[cols(length)] * 8
        + [cols(HALO + lags)] * 2
        + [cols(taps), cols(lags), const(part_f.shape), const(part_i.shape)],
        out_specs=[cols(length)] * 6 + [cols(HALO + lags)],
        out_shape=[shape(length, BF16)] * 6 + [shape(HALO + lags, BF16)],
        compiler_params=params,
        cost_estimate=pl.CostEstimate(flops=20_000_000_000, bytes_accessed=16_000_000, transcendentals=0),
    )(
        query_short, key_short, value_short, grad_short,
        query_medium, key_medium, value_medium, grad_medium,
        before, after, taps_short, taps_medium, jnp.asarray(part_f), jnp.asarray(part_i),
    )
    count = lax.axis_size("ctx")
    owners = min(count, channels // 128)
    width = channels // owners
    rows = HALO + lags
    dma = pltpu.SemaphoreType.DMA
    fl_b, bl_b, st_b, sums, square = pl.pallas_call(
        functools.partial(long_sums_kernel, count, owners),
        grid=(late,),
        in_specs=long_specs(early) + [pl.BlockSpec(memory_space=pl.ANY)],
        out_specs=[cols(length), cols(length), cols(3 * modes), const((owners, rows, width)), const((8, width))],
        out_shape=long_shapes(late)
        + [jax.ShapeDtypeStruct((owners, rows, width), BF16), jax.ShapeDtypeStruct((8, width), F32)],
        scratch_shapes=long_scratch
        + [
            pltpu.VMEM((count, rows, width), BF16),
            pltpu.VMEM((rows, width), BF16),
            pltpu.VMEM((owners, rows, width), BF16),
            dma,
        ]
        + [dma((count,))] * 4,
        compiler_params=pltpu.CompilerParams(
            dimension_semantics=("arbitrary",), vmem_limit_bytes=48 << 20,
            collective_id=1, has_side_effects=True,
        ),
    )(*long_in, outs[6])
    short_g, medium_g, residue_g, carries = exchange(
        jnp.concatenate([st_a, st_b], 1), sums, square, decay_rates, amplitudes, taps, lags, length
    )

    def early_cols(rows):
        return pl.BlockSpec((rows, block), lambda i: (0, jnp.minimum(i, early - 1)))

    def late_cols(rows):
        return pl.BlockSpec((rows, block), lambda i: (0, jnp.maximum(i - early, 0)))

    long_outs = pl.pallas_call(
        functools.partial(long_final_kernel, early),
        grid=grid,
        in_specs=[cols(length)] * 3
        + [early_cols(length), late_cols(length)] * 2
        + [cols(modes)] * 2
        + [cols(2 * modes)],
        out_specs=[cols(length)] * 3,
        out_shape=[shape(length, BF16)] * 3,
        scratch_shapes=[pltpu.VMEM((length, block), F32)] * 2,
        compiler_params=params,
        cost_estimate=pl.CostEstimate(flops=1_000_000_000, bytes_accessed=10_000_000, transcendentals=0),
    )(key_long, value_long, grad_long, fl_a, fl_b, bl_a, bl_b, weights, decay_rates, carries)
    return (*outs[:6], *long_outs, short_g, medium_g, residue_g)


def solution(mesh):
    tokens, filters = P("ctx", "ch"), P(None, "ch")
    return jax.shard_map(
        body,
        mesh=mesh,
        in_specs=(tokens,) * 12 + (filters,) * 4,
        out_specs=(tokens,) * 9 + (filters,) * 3,
        check_vma=False,
    )
```

```python
import functools

import jax
import jax.numpy as jnp
import numpy as np
from jax import lax
from jax.experimental import pallas as pl
from jax.experimental.pallas import tpu as pltpu
from jax.sharding import PartitionSpec as P

F32 = jnp.float32
BF16 = jnp.bfloat16
HALO = 16
MESH = pl.DeviceIdType.MESH


def from_behind(value, axis, steps):
    count = lax.axis_size(axis)
    first, last = (max(0, -steps), min(count, count - steps))
    return lax.ppermute(value, axis, [(source, source + steps) for source in range(first, last)])


def elementwise(first, second):
    return (first.astype(F32) * second.astype(F32)).astype(BF16)


def hi_lo(array):
    high = array.astype(BF16)
    low = (array - high.astype(F32)).astype(BF16)
    return high, low


def transform(size, points):
    turns = np.outer(2 * np.arange(size // 2) + 1, np.arange(points)) % (2 * size)
    angle = np.pi * turns / size
    return np.concatenate([np.cos(angle), np.sin(angle)], 0)


def np_hi_lo(matrix):
    matrix = np.asarray(matrix, np.float32)
    high = matrix.astype(jnp.bfloat16)
    low = (matrix - high.astype(np.float32)).astype(jnp.bfloat16)
    return np.stack([high, low])


def mul(first, second):
    return jnp.dot(first, second, preferred_element_type=F32)


def spectrum(matrix, data):
    return mul(matrix[0], data) + mul(matrix[1], data)


def wide(matrix, data):
    high, low = hi_lo(data)
    return mul(matrix[0], high) + (mul(matrix[0], low) + mul(matrix[1], high))


def inverse(matrix, data):
    high, low = hi_lo(data)
    return mul(matrix, high) + mul(matrix, low)


def convolved(first, second):
    half = first.shape[0] // 2
    fr, fs, sr, ss = first[:half], first[half:], second[:half], second[half:]
    return jnp.concatenate([fr * sr - fs * ss, fr * ss + fs * sr], 0)


def correlated(first, second):
    half = first.shape[0] // 2
    fr, fs, sr, ss = first[:half], first[half:], second[:half], second[half:]
    return jnp.concatenate([fr * sr + fs * ss, fs * sr - fr * ss], 0)


def ladder(rates):
    steps = lax.broadcasted_iota(jnp.int32, (1, 8, 1), 1).astype(F32)
    return jnp.exp(-rates[:, None, :] * steps), jnp.exp(-8.0 * rates)


def long_local_kernel(
    q_ref, k_ref, v_ref, g_ref, w_ref, d_ref, f_ref, i_ref, fl_ref, bl_ref, st_ref, h_scr, p_scr, s_scr
):
    length, width = q_ref.shape
    modes = d_ref.shape[0]
    tiles = length // 8
    product = elementwise(k_ref[...], v_ref[...])
    signal = elementwise(g_ref[...], q_ref[...])
    p_scr[...] = product.astype(F32)
    s_scr[...] = signal.astype(F32)
    for lane in range(0, width, 128):
        cols = slice(lane, lane + 128)
        rates = d_ref[:, cols]
        powers, step = ladder(rates)
        step = jnp.broadcast_to(step[:, None, :], (modes, 8, 128))

        def filter_step(a, state):
            h_scr[pl.ds(pl.multiple_of(a * 8, 8), 8), cols] = jnp.sum(state, 0)
            return state * step

        lax.fori_loop(0, tiles, filter_step, powers * w_ref[:, cols][:, None, :], unroll=8)
    ps = spectrum(f_ref, product)
    ss = spectrum(f_ref, signal)
    hs = wide(f_ref, h_scr[...])
    fl_ref[...] = inverse(i_ref[...], convolved(ps, hs))
    bl_ref[...] = inverse(i_ref[...], correlated(ss, hs))
    h_scr[...] = inverse(i_ref[...], correlated(ss, ps))
    for lane in range(0, width, 128):
        cols = slice(lane, lane + 128)
        rates = d_ref[:, cols]
        powers, step = ladder(rates)
        step = jnp.broadcast_to(step[:, None, :], (modes, 8, 128))
        steps = lax.broadcasted_iota(jnp.int32, (1, 8, 1), 1).astype(F32)
        falling = jnp.exp(-rates[:, None, :] * (7.0 - steps))
        zeros = jnp.zeros((modes, 8, 128), F32)

        def end_step(a, state):
            return state * step + p_scr[pl.ds(pl.multiple_of(a * 8, 8), 8), cols][None]

        def start_step(a, states):
            at = pl.ds(pl.multiple_of((tiles - 1 - a) * 8, 8), 8)
            return (states[0] * step + s_scr[at, cols][None], states[1] * step + h_scr[at, cols][None])

        ends = lax.fori_loop(0, tiles, end_step, zeros, unroll=8)
        st_ref[0:modes, cols] = jnp.sum(ends * falling, 1).astype(BF16)
        starts, lags = lax.fori_loop(0, tiles, start_step, (zeros, zeros), unroll=8)
        st_ref[modes : 2 * modes, cols] = jnp.sum(starts * powers, 1).astype(BF16)
        st_ref[2 * modes : 3 * modes, cols] = jnp.sum(lags * powers, 1).astype(BF16)


def explicit_kernel(
    qs, ks, vs, gs, qm, km, vm, gm, before, after, ts, tm, f_ref, i_ref,
    qs_o, ks_o, vs_o, qm_o, km_o, vm_o, raw_ref,
):
    length = qs.shape[0]
    taps = ts.shape[0]
    lags = tm.shape[0]
    product = elementwise(ks[...], vs[...]).astype(F32)
    signal = elementwise(gs[...], qs[...]).astype(F32)
    padded = jnp.concatenate([before[0:HALO].astype(F32), product], 0)
    trailing = jnp.concatenate([signal, after[0:HALO].astype(F32)], 0)
    forward = ts[0:1] * product
    backward = ts[0:1] * signal
    sums = [jnp.sum(signal * product, 0, keepdims=True)]
    for j in range(1, taps):
        shifted = padded[HALO - j : HALO - j + length]
        forward = forward + ts[j : j + 1] * shifted
        sums.append(jnp.sum(signal * shifted, 0, keepdims=True))
        backward = backward + ts[j : j + 1] * trailing[j : j + length]
    sums.append(jnp.zeros((HALO - taps, sums[0].shape[1]), F32))
    raw_ref[0:HALO, :] = jnp.concatenate(sums, 0).astype(BF16)
    qs_o[...] = (gs[...].astype(F32) * forward).astype(BF16)
    ks_o[...] = (backward * vs[...].astype(F32)).astype(BF16)
    vs_o[...] = (backward * ks[...].astype(F32)).astype(BF16)

    product = elementwise(km[...], vm[...])
    signal = elementwise(gm[...], qm[...])
    near = f_ref[:, :, 0:length]
    far = f_ref[:, :, length : length + lags]
    own = spectrum(near, product)
    ps = own - spectrum(far, before[HALO : HALO + lags])
    ss = spectrum(near, signal) + spectrum(far, after[HALO : HALO + lags])
    hs = wide(f_ref[:, :, 0:lags], tm[...])
    forward = inverse(i_ref[...], convolved(ps, hs))
    backward = inverse(i_ref[...], correlated(ss, hs))
    raw_ref[HALO : HALO + lags, :] = inverse(i_ref[0:lags], correlated(ss, own)).astype(BF16)
    qm_o[...] = (gm[...].astype(F32) * forward).astype(BF16)
    km_o[...] = (backward * vm[...].astype(F32)).astype(BF16)
    vm_o[...] = (backward * km[...].astype(F32)).astype(BF16)


def long_final_kernel(
    early, k_ref, v_ref, g_ref, fl_a, fl_b, bl_a, bl_b, w_ref, d_ref, c_ref, qo, ko, vo, f_scr, b_scr
):
    length, width = k_ref.shape
    modes = d_ref.shape[0]
    tiles = length // 8
    for lane in range(0, width, 128):
        cols = slice(lane, lane + 128)
        rates = d_ref[:, cols]
        powers, step = ladder(rates)
        step = jnp.broadcast_to(step[:, None, :], (modes, 8, 128))
        steps = lax.broadcasted_iota(jnp.int32, (1, 8, 1), 1).astype(F32)
        falling = jnp.exp(-rates[:, None, :] * (7.0 - steps))
        scale = w_ref[:, cols] * jnp.exp(-rates)
        into = (scale * c_ref[0:modes, cols])[:, None, :] * powers
        back = (scale * c_ref[modes : 2 * modes, cols])[:, None, :] * falling

        def one(a, states):
            f_scr[pl.ds(pl.multiple_of(a * 8, 8), 8), cols] = jnp.sum(states[0], 0)
            b_scr[pl.ds(pl.multiple_of((tiles - 1 - a) * 8, 8), 8), cols] = jnp.sum(states[1], 0)
            return (states[0] * step, states[1] * step)

        lax.fori_loop(0, tiles, one, (into, back), unroll=8)

    def finish(fl_ref, bl_ref):
        backward = bl_ref[...] + b_scr[...]
        qo[...] = (g_ref[...].astype(F32) * (fl_ref[...] + f_scr[...])).astype(BF16)
        ko[...] = (backward * v_ref[...].astype(F32)).astype(BF16)
        vo[...] = (backward * k_ref[...].astype(F32)).astype(BF16)

    first = pl.program_id(0) < early
    pl.when(first)(lambda: finish(fl_a, bl_a))
    pl.when(jnp.logical_not(first))(lambda: finish(fl_b, bl_b))


def guarded(always, condition, action):
    if always:
        action()
    else:
        pl.when(condition)(action)


def chunk(owner, width):
    return pl.ds(pl.multiple_of(owner * width, 128), width)


def peer_copy(source, target, k, send_sem, recv_sem, count, me):
    return pltpu.make_async_remote_copy(
        src_ref=source, dst_ref=target, send_sem=send_sem.at[k], recv_sem=recv_sem.at[k],
        device_id={"ctx": lax.rem(me + k, count)}, device_id_type=MESH,
    )


def long_sums_kernel(
    count, owners,
    q_ref, k_ref, v_ref, g_ref, w_ref, d_ref, f_ref, i_ref, raw,
    fl_ref, bl_ref, st_ref, sums_o, square_o,
    h_scr, p_scr, s_scr, in_raw, total_s, in_s,
    own_sem, raw_send, raw_recv, s_send, s_recv,
):
    me = lax.axis_index("ctx")
    step, steps = pl.program_id(0), pl.num_programs(0)
    width = in_raw.shape[2]
    every = owners == count

    def gathered(k, slot):
        source = raw.at[:, chunk(lax.rem(me + k, count), width)]
        return peer_copy(source, in_raw.at[slot], k, raw_send, raw_recv, count, me)

    def returned(k, slot):
        return peer_copy(total_s, in_s.at[slot], k, s_send, s_recv, count, me)

    def kept():
        return pltpu.make_async_copy(raw.at[:, chunk(me, width)], in_raw.at[me], own_sem)

    @pl.when(step == 0)
    def _():
        barrier = pltpu.get_barrier_semaphore()
        for k in range(1, count):
            pl.semaphore_signal(barrier, inc=1, device_id={"ctx": lax.rem(me + k, count)}, device_id_type=MESH)
        pl.semaphore_wait(barrier, count - 1)
        for k in range(1, count):
            guarded(every, lax.rem(me + k, count) < owners, lambda k=k: gathered(k, me).start())
        guarded(every, me < owners, lambda: kept().start())

    @pl.when(step == steps // 2)
    def _():
        def own():
            kept().wait()
            for k in range(1, count):
                gathered(k, lax.rem(me + count - k, count)).wait_recv()
            sums = in_raw[0].astype(F32)
            for i in range(1, count):
                sums = sums + in_raw[i].astype(F32)
            square = jnp.sum(jnp.sum(sums * sums, 0, keepdims=True), 1, keepdims=True)
            square_o[...] = jnp.broadcast_to(square, square_o.shape)
            total_s[...] = sums.astype(BF16)
            for k in range(1, count):
                returned(k, me).start()
            in_s[me] = total_s[...]

        if not every:
            square_o[...] = jnp.zeros(square_o.shape, F32)
        guarded(every, me < owners, own)

    long_local_kernel(
        q_ref, k_ref, v_ref, g_ref, w_ref, d_ref, f_ref, i_ref, fl_ref, bl_ref, st_ref, h_scr, p_scr, s_scr
    )

    @pl.when(step == steps - 1)
    def _():
        for k in range(1, count):
            source = lax.rem(me + count - k, count)
            guarded(every, source < owners, lambda k=k, source=source: returned(k, source).wait_recv())
        sums_o[...] = in_s[...]
        for k in range(1, count):
            guarded(every, lax.rem(me + k, count) < owners, lambda k=k: gathered(k, me).wait_send())
            guarded(every, me < owners, lambda k=k: returned(k, me).wait_send())


def exchange_kernel(
    count, groups, owners, length, entries,
    st, sums, square, rates, amp,
    short_o, medium_o, residue_o, carry_o,
    in_st, out_c, in_c, own_sq, in_sq,
    st_send, st_recv, c_send, c_recv, q_send, q_recv,
):
    me = lax.axis_index("ctx")
    group = lax.axis_index("ch")
    modes = rates.shape[0]
    lags = medium_o.shape[0]
    taps = short_o.shape[0]
    width = in_st.shape[2]
    every = owners == count

    barrier = pltpu.get_barrier_semaphore()
    for k in range(1, count):
        pl.semaphore_signal(barrier, inc=1, device_id={"ctx": lax.rem(me + k, count)}, device_id_type=MESH)
    for k in range(1, groups):
        pl.semaphore_signal(barrier, inc=1, device_id={"ch": lax.rem(group + k, groups)}, device_id_type=MESH)
    pl.semaphore_wait(barrier, count + groups - 2)

    def gathered(k, slot):
        source = st.at[:, chunk(lax.rem(me + k, count), width)]
        return peer_copy(source, in_st.at[slot], k, st_send, st_recv, count, me)

    def returned(k, slot):
        return peer_copy(out_c.at[lax.rem(me + k, count)], in_c.at[slot], k, c_send, c_recv, count, me)

    for k in range(1, count):
        guarded(every, lax.rem(me + k, count) < owners, lambda k=k: gathered(k, me).start())

    def own():
        in_st[me] = st[:, chunk(me, width)]
        rate = rates[:, chunk(me, width)]
        fade = jnp.exp(-rate)
        over = jnp.exp(-float(length) * rate)
        for k in range(1, count):
            gathered(k, lax.rem(me + count - k, count)).wait_recv()
        carry = jnp.zeros(rate.shape, F32)
        residue = jnp.zeros(rate.shape, F32)
        for i in range(count):
            out_c[i, 0:modes] = carry.astype(BF16)
            starts = in_st[i, modes : 2 * modes].astype(F32)
            residue = residue + in_st[i, 2 * modes : 3 * modes].astype(F32) + carry * fade * starts
            carry = carry * over + in_st[i, 0:modes].astype(F32)
        carry = jnp.zeros(rate.shape, F32)
        for i in reversed(range(count)):
            out_c[i, modes : 2 * modes] = carry.astype(BF16)
            carry = carry * over + in_st[i, modes : 2 * modes].astype(F32)
        residue = residue * amp[:, chunk(me, width)]
        total = jnp.sum(jnp.sum(residue * residue, 0, keepdims=True), 1, keepdims=True)
        total = jnp.broadcast_to(total, (8, width)) + square[...]
        parts = [part.astype(F32) for part in hi_lo(total)]
        shown = jnp.concatenate([residue] + parts, 0).astype(BF16)
        for i in range(count):
            out_c[i, 2 * modes : 3 * modes + 16] = shown
        for k in range(1, count):
            returned(k, me).start()
        in_c[me] = out_c[me]

    guarded(every, me < owners, own)

    for k in range(1, count):
        source = lax.rem(me + count - k, count)
        guarded(every, source < owners, lambda k=k, source=source: returned(k, source).wait_recv())
    total = jnp.zeros(own_sq.shape, F32)
    for i in range(owners):
        both = in_c[i, 3 * modes : 3 * modes + 16].astype(F32)
        total = total + (both[0:8] + both[8:16])
    own_sq[...] = total
    in_sq[group] = total

    def shared(k, slot):
        return pltpu.make_async_remote_copy(
            src_ref=own_sq, dst_ref=in_sq.at[slot], send_sem=q_send.at[k], recv_sem=q_recv.at[k],
            device_id={"ch": lax.rem(group + k, groups)}, device_id_type=MESH,
        )

    for k in range(1, groups):
        shared(k, group).start()
    for i in range(owners):
        carry_o[:, i * width : (i + 1) * width] = in_c[i, 0 : 2 * modes].astype(F32)
    for k in range(1, groups):
        shared(k, lax.rem(group + groups - k, groups)).wait_recv()
    total = in_sq[0]
    for i in range(1, groups):
        total = total + in_sq[i]
    factor = (1.0 / jnp.sqrt(total / entries + 1e-06))[0:1]
    for i in range(owners):
        cols = slice(i * width, (i + 1) * width)
        block = sums[i].astype(F32) * factor
        short_o[:, cols] = block[0:taps]
        medium_o[:, cols] = block[HALO : HALO + lags]
        residue_o[:, cols] = in_c[i, 2 * modes : 3 * modes].astype(F32) * factor
    for k in range(1, count):
        guarded(every, lax.rem(me + k, count) < owners, lambda k=k: gathered(k, me).wait_send())
        guarded(every, me < owners, lambda k=k: returned(k, me).wait_send())
    for k in range(1, groups):
        shared(k, group).wait_send()


def exchange(st, sums, square, rates, amp, taps, lags, length):
    count, groups = lax.axis_size("ctx"), lax.axis_size("ch")
    modes, wide_c = rates.shape
    owners, _, width = sums.shape
    entries = float((taps + lags + modes) * wide_c * groups)
    dma = pltpu.SemaphoreType.DMA
    vmem = pl.BlockSpec(memory_space=pltpu.VMEM)
    return pl.pallas_call(
        functools.partial(exchange_kernel, count, groups, owners, length, entries),
        out_shape=[
            jax.ShapeDtypeStruct((taps, wide_c), F32),
            jax.ShapeDtypeStruct((lags, wide_c), F32),
            jax.ShapeDtypeStruct((modes, wide_c), F32),
            jax.ShapeDtypeStruct((2 * modes, wide_c), F32),
        ],
        in_specs=[vmem] * 5,
        out_specs=[vmem] * 4,
        scratch_shapes=[
            pltpu.VMEM((count, 3 * modes, width), BF16),
            pltpu.VMEM((count, 3 * modes + 16, width), BF16),
            pltpu.VMEM((owners, 3 * modes + 16, width), BF16),
            pltpu.VMEM((8, width), F32),
            pltpu.VMEM((groups, 8, width), F32),
        ]
        + [dma((count,))] * 4
        + [dma((groups,))] * 2,
        compiler_params=pltpu.CompilerParams(
            collective_id=0, has_side_effects=True, vmem_limit_bytes=48 << 20
        ),
    )(st, sums, square, rates, amp)


def body(
    query_short, key_short, value_short, grad_short,
    query_medium, key_medium, value_medium, grad_medium,
    query_long, key_long, value_long, grad_long,
    taps_short, taps_medium, residues, decay_rates,
):
    length, channels = query_short.shape
    taps, lags, modes = taps_short.shape[0], taps_medium.shape[0], residues.shape[0]
    block = 256
    grid = (channels // block,)
    tails = jnp.concatenate(
        [
            elementwise(key_short[length - HALO :], value_short[length - HALO :]),
            elementwise(key_medium[length - lags :], value_medium[length - lags :]),
        ],
        0,
    )
    heads = jnp.concatenate(
        [
            elementwise(grad_short[:HALO], query_short[:HALO]),
            elementwise(grad_medium[:lags], query_medium[:lags]),
        ],
        0,
    )
    before = from_behind(tails, "ctx", 1)
    after = from_behind(heads, "ctx", -1)
    amplitudes = jnp.sqrt(-jnp.expm1(-2.0 * decay_rates))
    weights = amplitudes * residues

    def cols(rows):
        return pl.BlockSpec((rows, block), lambda i: (0, i))

    def const(shape):
        return pl.BlockSpec(shape, lambda i: (0,) * len(shape))

    def shape(rows, dtype):
        return jax.ShapeDtypeStruct((rows, channels), dtype)

    params = pltpu.CompilerParams(dimension_semantics=("arbitrary",), vmem_limit_bytes=48 << 20)
    full = 2 * length
    long_f = np_hi_lo(transform(full, length))
    long_i = np.asarray(transform(full, length).T * (2.0 / full), np.float32).astype(BF16)
    long_in = (
        query_long, key_long, value_long, grad_long, weights, decay_rates, jnp.asarray(long_f), jnp.asarray(long_i)
    )
    steps = channels // block
    early = steps * 3 // 8
    late = steps - early

    def part_cols(rows, first):
        return pl.BlockSpec((rows, block), lambda i: (0, i + first))

    def long_specs(first):
        return (
            [part_cols(length, first)] * 4
            + [part_cols(modes, first)] * 2
            + [const(long_f.shape), const(long_i.shape)]
        )

    def long_shapes(number):
        return [
            jax.ShapeDtypeStruct((rows, number * block), kind)
            for rows, kind in ((length, F32), (length, F32), (3 * modes, BF16))
        ]

    long_scratch = [pltpu.VMEM((length, block), F32)] * 3
    fl_a, bl_a, st_a = pl.pallas_call(
        long_local_kernel,
        grid=(early,),
        in_specs=long_specs(0),
        out_specs=[cols(length), cols(length), cols(3 * modes)],
        out_shape=long_shapes(early),
        scratch_shapes=long_scratch,
        compiler_params=params,
        cost_estimate=pl.CostEstimate(flops=10_000_000_000, bytes_accessed=4_000_000, transcendentals=0),
    )(*long_in)

    part = length + lags
    part_f = np_hi_lo(transform(part, part))
    part_i = np.asarray(transform(part, length).T * (2.0 / part), np.float32).astype(BF16)
    outs = pl.pallas_call(
        explicit_kernel,
        grid=grid,
        in_specs=[cols(length)] * 8
        + [cols(HALO + lags)] * 2
        + [cols(taps), cols(lags), const(part_f.shape), const(part_i.shape)],
        out_specs=[cols(length)] * 6 + [cols(HALO + lags)],
        out_shape=[shape(length, BF16)] * 6 + [shape(HALO + lags, BF16)],
        compiler_params=params,
        cost_estimate=pl.CostEstimate(flops=20_000_000_000, bytes_accessed=16_000_000, transcendentals=0),
    )(
        query_short, key_short, value_short, grad_short,
        query_medium, key_medium, value_medium, grad_medium,
        before, after, taps_short, taps_medium, jnp.asarray(part_f), jnp.asarray(part_i),
    )
    count = lax.axis_size("ctx")
    owners = min(count, channels // 128)
    width = channels // owners
    rows = HALO + lags
    dma = pltpu.SemaphoreType.DMA
    fl_b, bl_b, st_b, sums, square = pl.pallas_call(
        functools.partial(long_sums_kernel, count, owners),
        grid=(late,),
        in_specs=long_specs(early) + [pl.BlockSpec(memory_space=pl.ANY)],
        out_specs=[cols(length), cols(length), cols(3 * modes), const((owners, rows, width)), const((8, width))],
        out_shape=long_shapes(late)
        + [jax.ShapeDtypeStruct((owners, rows, width), BF16), jax.ShapeDtypeStruct((8, width), F32)],
        scratch_shapes=long_scratch
        + [
            pltpu.VMEM((count, rows, width), BF16),
            pltpu.VMEM((rows, width), BF16),
            pltpu.VMEM((owners, rows, width), BF16),
            dma,
        ]
        + [dma((count,))] * 4,
        compiler_params=pltpu.CompilerParams(
            dimension_semantics=("arbitrary",), vmem_limit_bytes=48 << 20,
            collective_id=1, has_side_effects=True,
        ),
    )(*long_in, outs[6])
    short_g, medium_g, residue_g, carries = exchange(
        jnp.concatenate([st_a, st_b], 1), sums, square, decay_rates, amplitudes, taps, lags, length
    )

    def early_cols(rows):
        return pl.BlockSpec((rows, block), lambda i: (0, jnp.minimum(i, early - 1)))

    def late_cols(rows):
        return pl.BlockSpec((rows, block), lambda i: (0, jnp.maximum(i - early, 0)))

    long_outs = pl.pallas_call(
        functools.partial(long_final_kernel, early),
        grid=grid,
        in_specs=[cols(length)] * 3
        + [early_cols(length), late_cols(length)] * 2
        + [cols(modes)] * 2
        + [cols(2 * modes)],
        out_specs=[cols(length)] * 3,
        out_shape=[shape(length, BF16)] * 3,
        scratch_shapes=[pltpu.VMEM((length, block), F32)] * 2,
        compiler_params=params,
        cost_estimate=pl.CostEstimate(flops=1_000_000_000, bytes_accessed=10_000_000, transcendentals=0),
    )(key_long, value_long, grad_long, fl_a, fl_b, bl_a, bl_b, weights, decay_rates, carries)
    return (*outs[:6], *long_outs, short_g, medium_g, residue_g)


def solution(mesh):
    tokens, filters = P("ctx", "ch"), P(None, "ch")
    return jax.shard_map(
        body,
        mesh=mesh,
        in_specs=(tokens,) * 12 + (filters,) * 4,
        out_specs=(tokens,) * 9 + (filters,) * 3,
        check_vma=False,
    )
```
